32 devices in a mesh: dp: 2 (over y), fsdp: 4 (over z), tensor: 4 (over x, core).
Axes of the slice: x: 2, y: 2, z: 4, core: 2. Of those that a mesh axis runs over, the one named last changes fastest.
Arguments:
- weight: float32 [4096, 4096], P('fsdp', 'tensor'), may hold values from -0.000234375 to 0.000234375
- momentum: bfloat16 [2, 4096, 4096], P('dp', 'fsdp', 'tensor'), may hold values from -8 to 8
- grads: bfloat16 [2, 2, 4096, 4096], P('dp', None, 'fsdp', 'tensor'), may hold values from -8 to 8
- right_factor: float32 [64, 4096], P(None, 'tensor'), may hold values from -1 to 1
Outputs:
- new_weight: float32 [4096, 4096], P('fsdp', 'tensor')
- new_momentum: bfloat16 [2, 4096, 4096], P('dp', 'fsdp', 'tensor')
- new_right: float32 [64, 4096], P(None, 'tensor')
The draws below stay inside these ranges and needn't reach their ends.
All inputs are finite; a program needn't handle non-finite values.
Results may differ from the reference program's by a relative error of at most 0.001.
Values sent between devices are 32-bit elements; how exact they have to be, the bound alone decides.
No kernel may reach another device: no remote copies, remote signals or barrier semaphores. Data moves between devices by JAX's collectives and lax.ppermute only.
A program may use at most 64 MiB of HBM per device.

```python
import math
import jax
import jax.numpy as jnp
from jax import lax

ROWS = 4096
COLS = 4096
RANK = 64
LOOPS = 2
REPLICAS = 2


noise_level = 0.35


def shared_basis(key):
    base = jax.random.fold_in(key, 101)
    subkeys = jax.random.split(base, 3)
    columns = jax.random.normal(subkeys[0], (ROWS, RANK), jnp.float32)
    basis_rows = jax.random.normal(subkeys[1], (RANK, COLS), jnp.float32)
    mixing = jax.random.normal(subkeys[2], (RANK, RANK), jnp.float32) * (0.25 / math.sqrt(RANK))
    return (columns, basis_rows, mixing)


def structured(key, marker, number):
    columns, basis_rows, mixing = shared_basis(key)
    subkeys = jax.random.split(jax.random.fold_in(key, marker), 3)
    scales = jnp.exp(jax.random.uniform(subkeys[0], (number, RANK), jnp.float32, -1.0, 1.0))
    own_part = jax.random.normal(subkeys[1], (number, RANK, RANK), jnp.float32) * (0.2 / math.sqrt(RANK))
    cores = own_part + mixing[None] + scales[:, :, None] * jnp.eye(RANK, dtype=jnp.float32)[None]
    noise_keys = jax.random.split(subkeys[2], number)

    def single(entry):
        core, noise_key = entry
        lowrank = jnp.dot(jnp.dot(columns, core), basis_rows) / math.sqrt(2 * RANK)
        noise = jax.random.normal(noise_key, (ROWS, COLS), jnp.float32) * noise_level
        return jnp.clip(lowrank + noise, -8.0, 8.0)
    return lax.map(single, (cores, noise_keys))


def draw_momentum(key, part):
    return structured(key, 1, REPLICAS).astype(jnp.bfloat16)


def draw_grads(key, part):
    values = structured(key, 2, REPLICAS * LOOPS)
    return values.reshape(REPLICAS, LOOPS, ROWS, COLS).astype(jnp.bfloat16)


def draw_right_factor(key, part):
    columns, basis_rows, mixing = shared_basis(key)
    subkeys = jax.random.split(jax.random.fold_in(key, 3), 3)
    jitter = jax.random.normal(subkeys[0], (RANK, COLS), jnp.float32)
    weights_common = jax.random.normal(subkeys[1], (RANK,), jnp.float32)
    common = jnp.dot(weights_common, basis_rows) / math.sqrt(RANK)
    lowest = -4.2
    spread = jnp.exp(jax.random.uniform(subkeys[2], (RANK, 1), jnp.float32, lowest, 0.0))
    blended_rows = common[None, :] + spread * (basis_rows + 0.5 * jitter)
    return blended_rows / jnp.sqrt(jnp.sum(blended_rows * blended_rows, axis=1, keepdims=True))


def steps_of(key, shape, cuts, smallest, largest):
    loudness = 1.0
    for dim, blocks in cuts:
        steps = jax.random.uniform(jax.random.fold_in(jax.random.fold_in(key, 6), dim), (blocks,), jnp.float32, smallest / len(cuts), largest / len(cuts))
        loudness = loudness * jnp.repeat(jnp.exp(steps), shape[dim] // blocks).reshape((-1,) + (1,) * (len(shape) - 1 - dim))
    return loudness


def centred(rng, extent, scale, bound, cuts=(), held_as=jnp.bfloat16):
    drawn = jax.random.normal(rng, extent, jnp.float32) * scale
    if len(cuts) > 0:
        drawn = steps_of(rng, extent, cuts, -0.22, 0.18) * drawn
    return jnp.clip(drawn, min=-bound, max=bound).astype(held_as)


def setup_inputs(seed: int = 0) -> dict:
    keys = jax.random.split(jax.random.key(seed), 5)
    weight = centred(keys[0], (ROWS, COLS), (0.02 * RANK ** 0.5 * COLS ** -1), 0.000234375, ((0, 4), (1, 4)), jnp.float32)
    momentum = draw_momentum(jax.random.fold_in(keys[4], 71), 0)
    grads = draw_grads(jax.random.fold_in(keys[4], 71), 0)
    right_factor = draw_right_factor(jax.random.fold_in(keys[4], 71), 0)
    return dict(weight=weight, momentum=momentum, grads=grads, right_factor=right_factor)


decay_part = 0.05
learn_rate = 0.02
epsilon = 1e-06

def orthonormal(factor):
    for sweep in range(2):
        gram = jnp.dot(factor.T.astype(jnp.float32), factor.astype(jnp.float32), precision=lax.Precision.HIGHEST, preferred_element_type=jnp.float32)
        lower = jnp.linalg.cholesky(gram)
        factor = jax.scipy.linalg.solve_triangular(lower, factor.T, lower=True).T
    return factor

def reference(weight, momentum, grads, right_factor):
    replicas = momentum.shape[0]
    blended = momentum.astype(jnp.float32) + lax.optimization_barrier(jnp.sum(grads.astype(jnp.float32), axis=1))
    left_raw = jnp.einsum('irc,kc->rk', blended, right_factor, precision=lax.Precision.HIGHEST) / replicas
    left = orthonormal(left_raw)
    right = jnp.einsum('irc,rk->ikc', blended, left, precision=lax.Precision.HIGHEST)
    new_momentum = (blended - decay_part * jnp.einsum('rk,ikc->irc', left, right, precision=lax.Precision.HIGHEST)).astype(jnp.bfloat16)
    shared = lax.optimization_barrier(jnp.sum(right, axis=0)) / replicas
    norms = jnp.sqrt(lax.optimization_barrier(jnp.sum(shared * shared, axis=1, keepdims=True)) + epsilon)
    new_right = shared / norms
    scale = learn_rate * math.sqrt(ROWS / COLS)
    new_weight = weight - scale * jnp.dot(left.astype(jnp.float32), new_right.astype(jnp.float32), precision=lax.Precision.HIGHEST, preferred_element_type=jnp.float32)
    return (new_weight, new_momentum, new_right)
```

```python
import functools
import math

import jax
import jax.numpy as jnp
from jax import lax
from jax.experimental import pallas as pl
from jax.experimental.pallas import tpu as pltpu
from jax.sharding import PartitionSpec as P

ROWS = 4096
COLS = 4096

decay_part = 0.05
learn_rate = 0.02
epsilon = 1e-06

F32 = jnp.float32
BF16 = jnp.bfloat16
NT = (((1,), (1,)), ((), ()))
NN = (((1,), (0,)), ((), ()))
TN = (((0,), (0,)), ((), ()))


def dot(a, b, dims=NN):
    return lax.dot_general(a, b, dims, preferred_element_type=F32)


def exact_dot(a, b, dims=NN):
    return lax.dot_general(
        a, b, dims, precision=lax.Precision.HIGHEST, preferred_element_type=F32
    )


def parts_of(x, count):
    parts = []
    for _ in range(count):
        part = x.astype(BF16)
        parts.append(part)
        x = x - part.astype(F32)
    return parts


def inverse_lower(gram, floor=None):
    rank = gram.shape[0]
    rows = lax.broadcasted_iota(jnp.int32, (rank, rank), 0)
    cols = lax.broadcasted_iota(jnp.int32, (rank, rank), 1)
    unit = jnp.where(rows == cols, 1.0, 0.0).astype(F32)
    both = jnp.concatenate([unit, gram], axis=1)
    height = 8
    full = (height, 2 * rank)
    blocks = [both[i : i + height] for i in range(0, rank, height)]
    sub = lax.broadcasted_iota(jnp.int32, full, 0)

    def spread(x, s):
        return jnp.broadcast_to(x[s : s + 1, :], full)

    if floor is not None:
        least = floor * jnp.sum(jnp.where(rows == cols, gram, 0.0), axis=1, keepdims=True)
        least = jnp.broadcast_to(least, (rank, 2 * rank))

    pivots = []
    for at in range(rank // height):
        live = blocks[at:]
        columns = []
        for j in range(height):
            k = rank + at * height + j
            columns.append(
                [jnp.where(sub >= 0, jnp.broadcast_to(x[:, k : k + 1], full), 0.0) for x in live]
            )
        found = jnp.ones(full, F32)
        for k in range(height):
            pivot = spread(columns[k][0], k)
            if floor is not None:
                pivot = jnp.maximum(pivot, spread(least[at * height : (at + 1) * height], k))
            found = jnp.where(sub == k, pivot, found)
            over = 1.0 / pivot
            line = spread(live[0], k) * over
            for j in range(k + 1, height):
                more = spread(columns[j][0], k) * over
                for i in range(len(live)):
                    columns[j][i] = columns[j][i] - columns[k][i] * more
            for i in range(len(live)):
                column = columns[k][i]
                if i == 0:
                    if k == height - 1:
                        continue
                    column = jnp.where(sub > k, column, 0.0)
                live[i] = live[i] - column * line
        blocks[at:] = live
        pivots.append(found)
    both = jnp.concatenate(blocks, axis=0)
    return both[:, :rank] / jnp.sqrt(jnp.concatenate(pivots, axis=0)[:, :rank])


VMEM_SPEC = pl.BlockSpec(memory_space=pltpu.VMEM)
SMEM_SPEC = pl.BlockSpec(memory_space=pltpu.SMEM)
ANY_SPEC = pl.BlockSpec(memory_space=pl.ANY)


GRANT = pltpu.CompilerParams(vmem_limit_bytes=20 * 1024 * 1024)


def held(x):
    return pltpu.with_memory_space_constraint(x, pltpu.VMEM)


def basis_kernel(r_ref, out_ref):
    out_ref[...] = inverse_lower(exact_dot(r_ref[...], r_ref[...], NT), 1e-5)


def basis(right_factor):
    rank = right_factor.shape[0]
    return pl.pallas_call(
        basis_kernel,
        out_shape=jax.ShapeDtypeStruct((rank, rank), F32),
        compiler_params=GRANT,
        name="basis",
    )(right_factor)


def raw_kernel(replicas, ids_ref, m_ref, g_ref, r_ref, out_ref):
    pieces, rank, height = out_ref.shape
    parts = jnp.concatenate(parts_of(r_ref[...], 3), axis=0)
    for piece in range(pieces):
        at = pl.ds(pl.multiple_of((ids_ref[0] * pieces + piece) * height, height), height)
        total = dot(parts, m_ref[0, at, :], NT)
        for i in range(g_ref.shape[1]):
            total += dot(parts, g_ref[0, i, at, :], NT)
        total = total[:rank] + total[rank : 2 * rank] + total[2 * rank :]
        out_ref[piece] = total / replicas


def raw_half(at, momentum, grads, right_factor, pieces, replicas):
    rank = right_factor.shape[0]
    height = grads.shape[2] // (2 * pieces)
    return pl.pallas_call(
        functools.partial(raw_kernel, replicas),
        out_shape=jax.ShapeDtypeStruct((pieces, rank, height), F32),
        in_specs=[SMEM_SPEC] + [VMEM_SPEC] * 3,
        out_specs=VMEM_SPEC,
        compiler_params=GRANT,
        name="raw_half",
    )(at, held(momentum), held(grads), right_factor)


def products_kernel(
    size, ids_ref, basis_ref, own_ref, other_ref, m_ref, g_ref, left_ref, *rest
):
    sends, (pieces_ref,) = rest[:size], rest[size:]
    half, rank, height = own_ref.shape
    cols = m_ref.shape[2]
    total = gram = None
    for q in range(2 * half):
        piece = jnp.where(ids_ref[0] == q // half, own_ref[q % half], other_ref[q % half])
        piece = exact_dot(basis_ref[...], piece)
        left_ref[q] = piece
        parts = jnp.concatenate(parts_of(piece, 3), axis=0)
        at = slice(q * height, (q + 1) * height)
        more = dot(parts, m_ref[0, at, :])
        for i in range(g_ref.shape[1]):
            more += dot(parts, g_ref[0, i, at, :])
        total = more if total is None else total + more
        more = exact_dot(piece, piece, NT)
        gram = more if gram is None else gram + more
    total = total[:rank] + total[rank : 2 * rank] + total[2 * rank :]
    width = cols // size
    for j in range(size):
        pieces_ref[j] = total[:, j * width : (j + 1) * width]
    for s, send in enumerate(sends):
        send[:rank, :] = pieces_ref[jnp.bitwise_xor(ids_ref[1], s)]
        pack(send, gram)


def pack(ref, gram):
    rank = gram.shape[0]
    side = ref.shape[1] // rank
    height = rank // side
    for j in range(side):
        ref[rank:, j * rank : (j + 1) * rank] = gram[j * height : (j + 1) * height]


def packed_rows(rank, width):
    side = width // rank
    assert side * rank == width and rank % side == 0
    return rank + rank // side


def products(ids, base, own, other, momentum, grads, size):
    half, rank, height = own.shape
    width = grads.shape[3] // size
    return pl.pallas_call(
        functools.partial(products_kernel, size),
        out_shape=[jax.ShapeDtypeStruct((2 * half, rank, height), F32)]
        + [jax.ShapeDtypeStruct((packed_rows(rank, width), width), F32)] * size,
        in_specs=[SMEM_SPEC] + [VMEM_SPEC] * 5,
        out_specs=[VMEM_SPEC] * (1 + size),
        scratch_shapes=[pltpu.VMEM((size, rank, width), F32)],
        compiler_params=GRANT,
        name="products",
    )(ids, base, own, other, held(momentum), held(grads))


def first_kernel(size, *refs):
    grams, left_ref, step_ref, first_ref, gram_ref = refs[:size], *refs[size:]
    rank = left_ref.shape[1]
    gram = grams[0][rank:, :]
    for ref in grams[1:]:
        gram = gram + ref[rank:, :]
    side = gram.shape[1] // rank
    gram = jnp.concatenate([gram[:, j * rank : (j + 1) * rank] for j in range(side)], axis=0)
    step = inverse_lower(gram)
    step_ref[...] = step
    total = None
    for q in range(left_ref.shape[0]):
        first = exact_dot(step, left_ref[q])
        first_ref[q] = first
        more = exact_dot(first, first, NT)
        total = more if total is None else total + more
    gram_ref[...] = total


def first_sweep(grams, left):
    rank = left.shape[1]
    square = jax.ShapeDtypeStruct((rank, rank), F32)
    return pl.pallas_call(
        functools.partial(first_kernel, len(grams)),
        out_shape=[square, jax.ShapeDtypeStruct(left.shape, F32), square],
        compiler_params=GRANT,
        name="first_sweep",
    )(*grams, left)


def second_kernel(size, replicas, *refs):
    grams, refs = refs[:size], refs[size:]
    own, other, refs = refs[:size], refs[size : 2 * size], refs[2 * size :]
    ids_ref, step_ref, first_ref, left_ref, both_ref, shared_ref, sums_ref = refs
    gram = grams[0][...]
    for ref in grams[1:]:
        gram = gram + ref[...]
    step = inverse_lower(gram)
    for q in range(first_ref.shape[0]):
        left_ref[q] = exact_dot(step, first_ref[q])
    both = exact_dot(step, step_ref[...])
    both_ref[...] = both
    sums = None
    for s in range(size):
        shared = exact_dot(both, own[s][...] + other[s][...]) / replicas
        shared_ref[jnp.bitwise_xor(ids_ref[1], s)] = shared
        squares = shared * shared
        lanes = min(128, squares.shape[1])
        for at in range(0, squares.shape[1], lanes):
            more = squares[:, at : at + lanes]
            sums = more if sums is None else sums + more
    sums_ref[...] = sums


def second_sweep(ids, grams, step, first, own, other, replicas):
    size = len(own)
    rank, width = own[0].shape
    square = jax.ShapeDtypeStruct((rank, rank), F32)
    return pl.pallas_call(
        functools.partial(second_kernel, size, replicas),
        out_shape=[
            jax.ShapeDtypeStruct(first.shape, F32),
            square,
            jax.ShapeDtypeStruct((size, rank, width), F32),
            jax.ShapeDtypeStruct((rank, min(128, width)), F32),
        ],
        in_specs=[VMEM_SPEC] * (3 * size) + [SMEM_SPEC] + [VMEM_SPEC] * 2,
        compiler_params=GRANT,
        name="second_sweep",
    )(*grams, *own, *other, ids, step, first)


def tall(x):
    hi, lo = parts_of(x, 2)
    return jnp.concatenate([hi, lo, hi, lo], axis=0)


def wide(x):
    hi, lo = parts_of(x, 2)
    return jnp.concatenate([hi, hi, lo, lo], axis=0)


def momentum_kernel(size, ids_ref, left_ref, both_ref, *refs):
    own, refs = refs[:size], refs[size:]
    m_ref, g_ref, out_ref, right_ref, slots_ref, sems = refs
    for s in range(size):
        right_ref[jnp.bitwise_xor(ids_ref[1], s)] = wide(exact_dot(both_ref[...], own[s][...]))
    width = right_ref.shape[2]
    pieces, rank, height = left_ref.shape
    copies = []
    for q in range(pieces):
        left = tall(left_ref[q])
        down = slice(q * height, (q + 1) * height)
        for j in range(size):
            at = slice(j * width, (j + 1) * width)
            blended = g_ref[0, 0, down, at].astype(F32)
            for i in range(1, g_ref.shape[1]):
                blended = blended + g_ref[0, i, down, at].astype(F32)
            blended = m_ref[0, down, at].astype(F32) + blended
            projected = dot(left, right_ref[j], TN)
            slots_ref[q, :, at] = (blended - decay_part * projected).astype(BF16)
        copies.append(
            pltpu.make_async_copy(slots_ref.at[q], out_ref.at[0, down, :], sems.at[q])
        )
        copies[-1].start()
    for copy in copies:
        copy.wait()


def momentum_step(ids, left, both, own, momentum, grads):
    size = len(own)
    pieces, rank, height = left.shape
    width = own[0].shape[1]
    cols = grads.shape[3]
    return pl.pallas_call(
        functools.partial(momentum_kernel, size),
        out_shape=jax.ShapeDtypeStruct(momentum.shape, BF16),
        in_specs=[SMEM_SPEC] + [VMEM_SPEC] * (4 + size),
        out_specs=ANY_SPEC,
        scratch_shapes=[
            pltpu.VMEM((size, 4 * rank, width), BF16),
            pltpu.VMEM((pieces, height, cols), BF16),
            pltpu.SemaphoreType.DMA((pieces,)),
        ],
        compiler_params=GRANT,
        name="momentum_step",
    )(ids, left, both, *own, held(momentum), held(grads))


def weight_kernel(count, scale, left_ref, shared_ref, *refs):
    sums, refs = refs[:count], refs[count:]
    w_ref, out_ref, new_right_ref, right_ref, slots_ref, sems = refs
    size, _, width = right_ref.shape
    total = sums[0][...]
    for ref in sums[1:]:
        total = total + ref[...]
    norm = jnp.sqrt(jnp.sum(total, axis=1, keepdims=True) + epsilon)
    for j in range(size):
        new_right = shared_ref[j] / norm
        new_right_ref[:, j * width : (j + 1) * width] = new_right
        right_ref[j] = wide(new_right)
    pieces, rank, height = left_ref.shape
    copies = []
    for q in range(pieces):
        left = tall(left_ref[q])
        down = slice(q * height, (q + 1) * height)
        for j in range(size):
            at = slice(j * width, (j + 1) * width)
            slots_ref[q, :, at] = w_ref[down, at] - scale * dot(left, right_ref[j], TN)
        copies.append(pltpu.make_async_copy(slots_ref.at[q], out_ref.at[down, :], sems.at[q]))
        copies[-1].start()
    for copy in copies:
        copy.wait()


def weight_step(left, shared, sums, weight, scale):
    pieces, rank, height = left.shape
    size, _, width = shared.shape
    rows, cols = weight.shape
    return pl.pallas_call(
        functools.partial(weight_kernel, len(sums), scale),
        out_shape=[
            jax.ShapeDtypeStruct(weight.shape, F32),
            jax.ShapeDtypeStruct((rank, cols), F32),
        ],
        in_specs=[VMEM_SPEC] * (3 + len(sums)),
        out_specs=[ANY_SPEC, VMEM_SPEC],
        scratch_shapes=[
            pltpu.VMEM((size, 4 * rank, width), BF16),
            pltpu.VMEM((pieces, height, cols), F32),
            pltpu.SemaphoreType.DMA((pieces,)),
        ],
        compiler_params=GRANT,
        name="weight_step",
    )(left, shared, *sums, held(weight))


def swap(x, axis, bit):
    size = lax.axis_size(axis)
    return lax.ppermute(x, axis, [(i, i ^ bit) for i in range(size)])


def bits_of(axis):
    size = lax.axis_size(axis)
    assert size & (size - 1) == 0
    return [(axis, 1 << i) for i in range(size.bit_length() - 1)]


def local(weight, momentum, grads, right_factor):
    replicas = lax.axis_size("dp")
    size = lax.axis_size("fsdp")
    near = lax.axis_index("tensor") % 2
    ids = jnp.stack([near, lax.axis_index("fsdp")]).astype(jnp.int32)

    raw = functools.partial(
        raw_half,
        momentum=momentum,
        grads=grads,
        right_factor=right_factor,
        pieces=2,
        replicas=replicas,
    )
    sent = swap(raw((1 - ids[:1])), "tensor", 1)
    kept = raw(ids[:1])
    total = kept + sent
    x, y = bits_of("tensor")[1:], bits_of("dp")
    a, b = total[0], total[1]
    for (ax, abit), (bx, bbit) in zip(x + y, y + x):
        a_in, b_in = swap(a, ax, abit), swap(b, bx, bbit)
        a, b = a + a_in, b + b_in
    own = jnp.stack([a, b])
    other = swap(own, "tensor", 1)

    left_raw, *sends = products(ids, basis(right_factor), own, other, momentum, grads, size)
    got = [sends[0]] + [swap(sends[s], "fsdp", s) for s in range(1, size)]
    rank = right_factor.shape[0]
    mine = sum(g[:rank] for g in got)
    pieces = [mine] + [swap(mine, "fsdp", s) for s in range(1, size)]

    step, first, gram = first_sweep(got, left_raw)
    grams = [gram] + [swap(gram, "fsdp", s) for s in range(1, size)]

    here, rest = mine, jnp.stack(pieces[1:])
    for axis, bit in y[:-1]:
        here = here + swap(here, axis, bit)
        rest = rest + swap(rest, axis, bit)
    axis, bit = y[-1]
    here_in, rest_in = swap(here, axis, bit), swap(rest, axis, bit)
    ours = [here] + [rest[s] for s in range(size - 1)]
    theirs = [here_in] + [rest_in[s] for s in range(size - 1)]

    left, both, shared, sums = second_sweep(ids, grams, step, first, ours, theirs, replicas)
    sums_all = [sums] + [swap(sums, "tensor", s) for s in range(1, lax.axis_size("tensor"))]
    new_momentum = momentum_step(ids, left, both, pieces, momentum, grads)
    scale = learn_rate * math.sqrt(ROWS / COLS)
    new_weight, new_right = weight_step(left, shared, sums_all, weight, scale)
    return (new_weight, new_momentum, new_right)


def solution(mesh):
    placed = (
        P("fsdp", "tensor"),
        P("dp", "fsdp", "tensor"),
        P("dp", None, "fsdp", "tensor"),
        P(None, "tensor"),
    )
    return jax.shard_map(
        local,
        mesh=mesh,
        in_specs=placed,
        out_specs=(P("fsdp", "tensor"), P("dp", "fsdp", "tensor"), P(None, "tensor")),
        check_vma=False,
    )
```

```python
import functools
import math

import jax
import jax.numpy as jnp
from jax import lax
from jax.experimental import pallas as pl
from jax.experimental.pallas import tpu as pltpu
from jax.sharding import PartitionSpec as P


ROWS = 4096
COLS = 4096

decay_part = 0.05
learn_rate = 0.02
epsilon = 1e-06

F32 = jnp.float32
BF16 = jnp.bfloat16
NT = (((1,), (1,)), ((), ()))
NN = (((1,), (0,)), ((), ()))
TN = (((0,), (0,)), ((), ()))


def dot(a, b, dims=NN):
    return lax.dot_general(a, b, dims, preferred_element_type=F32)


def exact_dot(a, b, dims=NN):
    return lax.dot_general(
        a, b, dims, precision=lax.Precision.HIGHEST, preferred_element_type=F32
    )


def parts_of(x, count):
    parts = []
    for _ in range(count):
        part = x.astype(BF16)
        parts.append(part)
        x = x - part.astype(F32)
    return parts


def inverse_lower(gram, floor=None):
    rank = gram.shape[0]
    rows = lax.broadcasted_iota(jnp.int32, (rank, rank), 0)
    cols = lax.broadcasted_iota(jnp.int32, (rank, rank), 1)
    unit = jnp.where(rows == cols, 1.0, 0.0).astype(F32)
    both = jnp.concatenate([unit, gram], axis=1)
    height = 8
    full = (height, 2 * rank)
    blocks = [both[i : i + height] for i in range(0, rank, height)]
    sub = lax.broadcasted_iota(jnp.int32, full, 0)

    def spread(x, s):
        return jnp.broadcast_to(x[s : s + 1, :], full)

    if floor is not None:
        least = floor * jnp.sum(jnp.where(rows == cols, gram, 0.0), axis=1, keepdims=True)
        least = jnp.broadcast_to(least, (rank, 2 * rank))

    pivots = []
    for at in range(rank // height):
        live = blocks[at:]
        columns = []
        for j in range(height):
            k = rank + at * height + j
            columns.append(
                [jnp.where(sub >= 0, jnp.broadcast_to(x[:, k : k + 1], full), 0.0) for x in live]
            )
        found = jnp.ones(full, F32)
        for k in range(height):
            pivot = spread(columns[k][0], k)
            if floor is not None:
                pivot = jnp.maximum(pivot, spread(least[at * height : (at + 1) * height], k))
            found = jnp.where(sub == k, pivot, found)
            over = 1.0 / pivot
            line = spread(live[0], k) * over
            for j in range(k + 1, height):
                more = spread(columns[j][0], k) * over
                for i in range(len(live)):
                    columns[j][i] = columns[j][i] - columns[k][i] * more
            for i in range(len(live)):
                column = columns[k][i]
                if i == 0:
                    if k == height - 1:
                        continue
                    column = jnp.where(sub > k, column, 0.0)
                live[i] = live[i] - column * line
        blocks[at:] = live
        pivots.append(found)
    both = jnp.concatenate(blocks, axis=0)
    return both[:, :rank] / jnp.sqrt(jnp.concatenate(pivots, axis=0)[:, :rank])


VMEM_SPEC = pl.BlockSpec(memory_space=pltpu.VMEM)
SMEM_SPEC = pl.BlockSpec(memory_space=pltpu.SMEM)
HBM_SPEC = pl.BlockSpec(memory_space=pltpu.HBM)


GRANT = pltpu.CompilerParams(vmem_limit_bytes=20 * 1024 * 1024)


def left_out(x):
    return pltpu.with_memory_space_constraint(x, pltpu.HBM)


def held(x):
    return pltpu.with_memory_space_constraint(x, pltpu.VMEM)


def raw_terms(parts, m_ref, g_ref, at):
    rank = parts.shape[0] // 3
    total = dot(parts, m_ref[0, at, :], NT)
    for i in range(g_ref.shape[1]):
        total += dot(parts, g_ref[0, i, at, :], NT)
    return total[:rank] + total[rank : 2 * rank] + total[2 * rank :]


def rows_of(half, piece, pieces, height):
    return pl.ds(pl.multiple_of((half * pieces + piece) * height, height), height)


def load_kernel(
    replicas, ids_ref, m_hbm, g_hbm, r_hbm, m_ref, g_ref, r_ref, parts_ref, out_ref, sems, r_sem
):
    pieces, _, height = out_ref.shape
    loops = g_hbm.shape[1]
    first = pltpu.make_async_copy(r_hbm, r_ref, r_sem)
    first.start()
    copies = []
    for piece in range(2 * pieces):
        half = ids_ref[0] if piece >= pieces else 1 - ids_ref[0]
        at = rows_of(half, piece % pieces, pieces, height)
        group = [
            pltpu.make_async_copy(m_hbm.at[0, at, :], m_ref.at[0, at, :], sems.at[piece, loops])
        ]
        for i in range(loops):
            group.append(
                pltpu.make_async_copy(
                    g_hbm.at[0, i, at, :], g_ref.at[0, i, at, :], sems.at[piece, i]
                )
            )
        for copy in group:
            copy.start()
        copies.append(group)
    first.wait()
    parts = jnp.concatenate(parts_of(r_ref[...], 3), axis=0)
    parts_ref[...] = parts
    for piece in range(pieces):
        for copy in copies[piece]:
            copy.wait()
        at = rows_of(1 - ids_ref[0], piece, pieces, height)
        out_ref[piece] = raw_terms(parts, m_ref, g_ref, at) / replicas
    for group in copies[pieces:]:
        for copy in group:
            copy.wait()


def load(ids, momentum, grads, right_factor, pieces, replicas):
    rank, cols = right_factor.shape
    loops, rows = grads.shape[1:3]
    return pl.pallas_call(
        functools.partial(load_kernel, replicas),
        out_shape=[
            pltpu.VMEM(momentum.shape, momentum.dtype),
            pltpu.VMEM(grads.shape, grads.dtype),
            pltpu.VMEM((rank, cols), F32),
            pltpu.VMEM((3 * rank, cols), BF16),
            jax.ShapeDtypeStruct((pieces, rank, rows // (2 * pieces)), F32),
        ],
        in_specs=[SMEM_SPEC] + [HBM_SPEC] * 3,
        out_specs=[VMEM_SPEC] * 5,
        scratch_shapes=[
            pltpu.SemaphoreType.DMA((2 * pieces, loops + 1)),
            pltpu.SemaphoreType.DMA,
        ],
        compiler_params=GRANT,
        name="load",
    )(ids, left_out(momentum), left_out(grads), left_out(right_factor))


def basis_kernel(r_ref, out_ref):
    out_ref[...] = inverse_lower(exact_dot(r_ref[...], r_ref[...], NT), 1e-5)


def basis(right_factor):
    rank = right_factor.shape[0]
    return pl.pallas_call(
        basis_kernel,
        out_shape=jax.ShapeDtypeStruct((rank, rank), F32),
        in_specs=[VMEM_SPEC],
        out_specs=VMEM_SPEC,
        compiler_params=GRANT,
        name="basis",
    )(held(right_factor))


def raw_kernel(replicas, ids_ref, m_ref, g_ref, parts_ref, out_ref):
    pieces, _, height = out_ref.shape
    parts = parts_ref[...]
    for piece in range(pieces):
        at = rows_of(ids_ref[0], piece, pieces, height)
        out_ref[piece] = raw_terms(parts, m_ref, g_ref, at) / replicas


def raw_half(ids, momentum, grads, parts, pieces, replicas):
    rank = parts.shape[0] // 3
    height = grads.shape[2] // (2 * pieces)
    return pl.pallas_call(
        functools.partial(raw_kernel, replicas),
        out_shape=jax.ShapeDtypeStruct((pieces, rank, height), F32),
        in_specs=[SMEM_SPEC] + [VMEM_SPEC] * 3,
        out_specs=VMEM_SPEC,
        compiler_params=GRANT,
        name="raw_half",
    )(ids, held(momentum), held(grads), held(parts))


def products_kernel(
    size, ids_ref, basis_ref, own_ref, other_ref, m_ref, g_ref, left_ref, *rest
):
    sends, (pieces_ref,) = rest[:size], rest[size:]
    half, rank, height = own_ref.shape
    cols = m_ref.shape[2]
    total = gram = None
    for q in range(2 * half):
        piece = jnp.where(ids_ref[0] == q // half, own_ref[q % half], other_ref[q % half])
        piece = exact_dot(basis_ref[...], piece)
        left_ref[q] = piece
        parts = jnp.concatenate(parts_of(piece, 3), axis=0)
        at = slice(q * height, (q + 1) * height)
        more = dot(parts, m_ref[0, at, :])
        for i in range(g_ref.shape[1]):
            more += dot(parts, g_ref[0, i, at, :])
        total = more if total is None else total + more
        more = exact_dot(piece, piece, NT)
        gram = more if gram is None else gram + more
    total = total[:rank] + total[rank : 2 * rank] + total[2 * rank :]
    width = cols // size
    for j in range(size):
        pieces_ref[j] = total[:, j * width : (j + 1) * width]
    for s, send in enumerate(sends):
        send[:rank, :] = pieces_ref[jnp.bitwise_xor(ids_ref[1], s)]
        pack(send, gram)


def pack(ref, gram):
    rank = gram.shape[0]
    side = ref.shape[1] // rank
    height = rank // side
    for j in range(side):
        ref[rank:, j * rank : (j + 1) * rank] = gram[j * height : (j + 1) * height]


def packed_rows(rank, width):
    side = width // rank
    assert side * rank == width and rank % side == 0
    return rank + rank // side


def products(ids, base, own, other, momentum, grads, size):
    half, rank, height = own.shape
    width = grads.shape[3] // size
    return pl.pallas_call(
        functools.partial(products_kernel, size),
        out_shape=[jax.ShapeDtypeStruct((2 * half, rank, height), F32)]
        + [jax.ShapeDtypeStruct((packed_rows(rank, width), width), F32)] * size,
        in_specs=[SMEM_SPEC] + [VMEM_SPEC] * 5,
        out_specs=[VMEM_SPEC] * (1 + size),
        scratch_shapes=[pltpu.VMEM((size, rank, width), F32)],
        compiler_params=GRANT,
        name="products",
    )(ids, base, own, other, held(momentum), held(grads))


def first_kernel(size, *refs):
    grams, left_ref, step_ref, first_ref, gram_ref = refs[:size], *refs[size:]
    rank = left_ref.shape[1]
    gram = grams[0][rank:, :]
    for ref in grams[1:]:
        gram = gram + ref[rank:, :]
    side = gram.shape[1] // rank
    gram = jnp.concatenate([gram[:, j * rank : (j + 1) * rank] for j in range(side)], axis=0)
    step = inverse_lower(gram)
    step_ref[...] = step
    total = None
    for q in range(left_ref.shape[0]):
        first = exact_dot(step, left_ref[q])
        first_ref[q] = first
        more = exact_dot(first, first, NT)
        total = more if total is None else total + more
    gram_ref[...] = total


def first_sweep(grams, left):
    rank = left.shape[1]
    square = jax.ShapeDtypeStruct((rank, rank), F32)
    return pl.pallas_call(
        functools.partial(first_kernel, len(grams)),
        out_shape=[square, jax.ShapeDtypeStruct(left.shape, F32), square],
        compiler_params=GRANT,
        name="first_sweep",
    )(*grams, left)


def second_kernel(size, *refs):
    grams, (step_ref, first_ref, left_ref, both_ref) = refs[:size], refs[size:]
    gram = grams[0][...]
    for ref in grams[1:]:
        gram = gram + ref[...]
    step = inverse_lower(gram)
    for q in range(first_ref.shape[0]):
        left_ref[q] = exact_dot(step, first_ref[q])
    both_ref[...] = exact_dot(step, step_ref[...])


def second_sweep(grams, step, first):
    return pl.pallas_call(
        functools.partial(second_kernel, len(grams)),
        out_shape=[
            jax.ShapeDtypeStruct(first.shape, F32),
            jax.ShapeDtypeStruct(step.shape, F32),
        ],
        compiler_params=GRANT,
        name="second_sweep",
    )(*grams, step, first)


def shared_kernel(size, replicas, ids_ref, both_ref, *refs):
    own, other, (shared_ref, sums_ref) = refs[:size], refs[size : 2 * size], refs[2 * size :]
    both = both_ref[...]
    sums = None
    for s in range(size):
        shared = exact_dot(both, own[s][...] + other[s][...]) / replicas
        shared_ref[jnp.bitwise_xor(ids_ref[1], s)] = shared
        squares = shared * shared
        lanes = min(128, squares.shape[1])
        for at in range(0, squares.shape[1], lanes):
            more = squares[:, at : at + lanes]
            sums = more if sums is None else sums + more
    sums_ref[...] = sums


def shared_step(ids, both, own, other, replicas):
    size = len(own)
    rank, width = own[0].shape
    return pl.pallas_call(
        functools.partial(shared_kernel, size, replicas),
        out_shape=[
            jax.ShapeDtypeStruct((size, rank, width), F32),
            jax.ShapeDtypeStruct((rank, min(128, width)), F32),
        ],
        in_specs=[SMEM_SPEC] + [VMEM_SPEC] * (1 + 2 * size),
        out_specs=[VMEM_SPEC] * 2,
        compiler_params=GRANT,
        name="shared_step",
    )(ids, both, *own, *other)


def tall(x):
    hi, lo = parts_of(x, 2)
    return jnp.concatenate([hi, lo, hi, lo], axis=0)


def wide(x):
    hi, lo = parts_of(x, 2)
    return jnp.concatenate([hi, hi, lo, lo], axis=0)


def momentum_kernel(size, ids_ref, left_ref, both_ref, *refs):
    own, refs = refs[:size], refs[size:]
    m_ref, g_ref, out_ref, right_ref, slots_ref, sems = refs
    for s in range(size):
        right_ref[jnp.bitwise_xor(ids_ref[1], s)] = wide(exact_dot(both_ref[...], own[s][...]))
    width = right_ref.shape[2]
    pieces, _, height = left_ref.shape
    copies = []
    for q in range(pieces):
        left = tall(left_ref[q])
        down = slice(q * height, (q + 1) * height)
        for j in range(size):
            at = slice(j * width, (j + 1) * width)
            blended = g_ref[0, 0, down, at].astype(F32)
            for i in range(1, g_ref.shape[1]):
                blended = blended + g_ref[0, i, down, at].astype(F32)
            blended = m_ref[0, down, at].astype(F32) + blended
            projected = dot(left, right_ref[j], TN)
            slots_ref[q, :, at] = (blended - decay_part * projected).astype(BF16)
        copies.append(
            pltpu.make_async_copy(slots_ref.at[q], out_ref.at[0, down, :], sems.at[q])
        )
        copies[-1].start()
    for copy in copies:
        copy.wait()


def momentum_step(ids, left, both, own, momentum, grads):
    size = len(own)
    pieces, rank, height = left.shape
    width = own[0].shape[1]
    cols = grads.shape[3]
    return pl.pallas_call(
        functools.partial(momentum_kernel, size),
        out_shape=jax.ShapeDtypeStruct(momentum.shape, BF16),
        in_specs=[SMEM_SPEC] + [VMEM_SPEC] * (4 + size),
        out_specs=HBM_SPEC,
        scratch_shapes=[
            pltpu.VMEM((size, 4 * rank, width), BF16),
            pltpu.VMEM((pieces, height, cols), BF16),
            pltpu.SemaphoreType.DMA((pieces,)),
        ],
        compiler_params=GRANT,
        name="momentum_step",
    )(ids, left, both, *own, held(momentum), held(grads))


def weight_kernel(count, scale, left_ref, shared_ref, *refs):
    sums, refs = refs[:count], refs[count:]
    w_ref, out_ref, new_right_ref, right_ref, slots_ref, sems = refs
    size, _, width = right_ref.shape
    total = sums[0][...]
    for ref in sums[1:]:
        total = total + ref[...]
    norm = jnp.sqrt(jnp.sum(total, axis=1, keepdims=True) + epsilon)
    for j in range(size):
        new_right = shared_ref[j] / norm
        new_right_ref[:, j * width : (j + 1) * width] = new_right
        right_ref[j] = wide(new_right)
    pieces, _, height = left_ref.shape
    copies = []
    for q in range(pieces):
        left = tall(left_ref[q])
        down = slice(q * height, (q + 1) * height)
        for j in range(size):
            at = slice(j * width, (j + 1) * width)
            slots_ref[q, :, at] = w_ref[down, at] - scale * dot(left, right_ref[j], TN)
        copies.append(pltpu.make_async_copy(slots_ref.at[q], out_ref.at[down, :], sems.at[q]))
        copies[-1].start()
    for copy in copies:
        copy.wait()


def weight_step(left, shared, sums, weight, scale):
    pieces, rank, height = left.shape
    size, _, width = shared.shape
    _, cols = weight.shape
    return pl.pallas_call(
        functools.partial(weight_kernel, len(sums), scale),
        out_shape=[
            jax.ShapeDtypeStruct(weight.shape, F32),
            jax.ShapeDtypeStruct((rank, cols), F32),
        ],
        in_specs=[VMEM_SPEC] * (3 + len(sums)),
        out_specs=[HBM_SPEC, VMEM_SPEC],
        scratch_shapes=[
            pltpu.VMEM((size, 4 * rank, width), BF16),
            pltpu.VMEM((pieces, height, cols), F32),
            pltpu.SemaphoreType.DMA((pieces,)),
        ],
        compiler_params=GRANT,
        name="weight_step",
    )(left, shared, *sums, held(weight))


def swap(x, axis, bit):
    size = lax.axis_size(axis)
    return lax.ppermute(x, axis, [(i, i ^ bit) for i in range(size)])


def bits_of(axis):
    size = lax.axis_size(axis)
    assert size & (size - 1) == 0
    return [(axis, 1 << i) for i in range(size.bit_length() - 1)]


def step(weight, momentum, grads, right_factor):
    replicas = lax.axis_size("dp")
    size = lax.axis_size("fsdp")
    others = range(1, size)
    rank = right_factor.shape[0]
    near = lax.axis_index("tensor") % 2
    ids = jnp.stack([near, lax.axis_index("fsdp")]).astype(jnp.int32)

    momentum, grads, right_factor, parts, sent = load(
        ids, momentum, grads, right_factor, 2, replicas
    )
    sent = swap(sent, "tensor", 1)
    kept = raw_half(ids, momentum, grads, parts, 2, replicas)
    own = kept + sent
    right_factor, own = lax.optimization_barrier((right_factor, own))
    base = basis(right_factor)
    for axis, bit in bits_of("tensor")[1:] + bits_of("dp"):
        own = own + swap(own, axis, bit)
    other = swap(own, "tensor", 1)

    left_raw, *sends = products(ids, base, own, other, momentum, grads, size)
    got = [sends[0]] + [swap(sends[s], "fsdp", s) for s in others]
    mine = sum(g[:rank] for g in got)
    pieces = [mine] + [swap(mine, "fsdp", s) for s in others]

    weight, left_raw = lax.optimization_barrier((weight, left_raw))
    factor, first, gram = first_sweep(got, left_raw)
    grams = [gram] + [swap(gram, "fsdp", s) for s in others]

    ours, theirs = [], []
    for piece in pieces:
        for axis, bit in bits_of("dp")[:-1]:
            piece = piece + swap(piece, axis, bit)
        ours.append(piece)
        theirs.append(swap(piece, *bits_of("dp")[-1]))

    left, both = second_sweep(grams, factor, first)
    shared, sums = shared_step(ids, both, ours, theirs, replicas)
    sums_all = [sums] + [swap(sums, "tensor", s) for s in range(1, lax.axis_size("tensor"))]
    new_momentum = momentum_step(ids, left, both, pieces, momentum, grads)
    scale = learn_rate * math.sqrt(ROWS / COLS)
    new_weight, new_right = weight_step(left, shared, sums_all, weight, scale)
    return (new_weight, new_momentum, new_right)


def solution(mesh):
    placed = (
        P("fsdp", "tensor"),
        P("dp", "fsdp", "tensor"),
        P("dp", None, "fsdp", "tensor"),
        P(None, "tensor"),
    )
    return jax.shard_map(
        step,
        mesh=mesh,
        in_specs=placed,
        out_specs=(P("fsdp", "tensor"), P("dp", "fsdp", "tensor"), P(None, "tensor")),
        check_vma=False,
    )
```

```python
import functools
import math

import jax
import jax.numpy as jnp
from jax import lax
from jax.experimental import pallas as pl
from jax.experimental.pallas import tpu as pltpu
from jax.sharding import PartitionSpec as P


ROWS = 4096
COLS = 4096

decay_part = 0.05
learn_rate = 0.02
epsilon = 1e-06

F32 = jnp.float32
BF16 = jnp.bfloat16
NT = (((1,), (1,)), ((), ()))
NN = (((1,), (0,)), ((), ()))
TN = (((0,), (0,)), ((), ()))


def dot(a, b, dims=NN):
    return lax.dot_general(a, b, dims, preferred_element_type=F32)


def exact_dot(a, b, dims=NN):
    return lax.dot_general(
        a, b, dims, precision=lax.Precision.HIGHEST, preferred_element_type=F32
    )


def parts_of(x, count):
    parts = []
    for _ in range(count):
        part = x.astype(BF16)
        parts.append(part)
        x = x - part.astype(F32)
    return parts


def inverse_lower(gram, floor=None):
    rank = gram.shape[0]
    rows = lax.broadcasted_iota(jnp.int32, (rank, rank), 0)
    cols = lax.broadcasted_iota(jnp.int32, (rank, rank), 1)
    unit = jnp.where(rows == cols, 1.0, 0.0).astype(F32)
    both = jnp.concatenate([unit, gram], axis=1)
    height = 8
    full = (height, 2 * rank)
    blocks = [both[i : i + height] for i in range(0, rank, height)]
    sub = lax.broadcasted_iota(jnp.int32, full, 0)

    def spread(x, s):
        return jnp.broadcast_to(x[s : s + 1, :], full)

    if floor is not None:
        least = floor * jnp.sum(jnp.where(rows == cols, gram, 0.0), axis=1, keepdims=True)
        least = jnp.broadcast_to(least, (rank, 2 * rank))

    pivots = []
    for at in range(rank // height):
        live = blocks[at:]
        columns = []
        for j in range(height):
            k = rank + at * height + j
            columns.append(
                [jnp.where(sub >= 0, jnp.broadcast_to(x[:, k : k + 1], full), 0.0) for x in live]
            )
        found = jnp.ones(full, F32)
        for k in range(height):
            pivot = spread(columns[k][0], k)
            if floor is not None:
                pivot = jnp.maximum(pivot, spread(least[at * height : (at + 1) * height], k))
            found = jnp.where(sub == k, pivot, found)
            over = 1.0 / pivot
            line = spread(live[0], k) * over
            for j in range(k + 1, height):
                more = spread(columns[j][0], k) * over
                for i in range(len(live)):
                    columns[j][i] = columns[j][i] - columns[k][i] * more
            for i in range(len(live)):
                column = columns[k][i]
                if i == 0:
                    if k == height - 1:
                        continue
                    column = jnp.where(sub > k, column, 0.0)
                live[i] = live[i] - column * line
        blocks[at:] = live
        pivots.append(found)
    both = jnp.concatenate(blocks, axis=0)
    return both[:, :rank] / jnp.sqrt(jnp.concatenate(pivots, axis=0)[:, :rank])


VMEM_SPEC = pl.BlockSpec(memory_space=pltpu.VMEM)
SMEM_SPEC = pl.BlockSpec(memory_space=pltpu.SMEM)
HBM_SPEC = pl.BlockSpec(memory_space=pltpu.HBM)


GRANT = pltpu.CompilerParams(vmem_limit_bytes=20 * 1024 * 1024)


def left_out(x):
    return pltpu.with_memory_space_constraint(x, pltpu.HBM)


def held(x):
    return pltpu.with_memory_space_constraint(x, pltpu.VMEM)


def raw_terms(parts, m_ref, g_ref, at):
    rank = parts.shape[0] // 3
    total = dot(parts, m_ref[0, at, :], NT)
    for i in range(g_ref.shape[1]):
        total += dot(parts, g_ref[0, i, at, :], NT)
    return total[:rank] + total[rank : 2 * rank] + total[2 * rank :]


def rows_of(half, piece, pieces, height):
    return pl.ds(pl.multiple_of((half * pieces + piece) * height, height), height)


def load_kernel(
    replicas, ids_ref, m_hbm, g_hbm, r_hbm, m_ref, g_ref, r_ref, out_ref, sems, r_sem
):
    pieces, _, height = out_ref.shape
    loops = g_hbm.shape[1]
    first = pltpu.make_async_copy(r_hbm, r_ref, r_sem)
    first.start()
    copies = []
    for piece in range(2 * pieces):
        half = ids_ref[0] if piece >= pieces else 1 - ids_ref[0]
        at = rows_of(half, piece % pieces, pieces, height)
        group = [
            pltpu.make_async_copy(m_hbm.at[0, at, :], m_ref.at[0, at, :], sems.at[piece, loops])
        ]
        for i in range(loops):
            group.append(
                pltpu.make_async_copy(
                    g_hbm.at[0, i, at, :], g_ref.at[0, i, at, :], sems.at[piece, i]
                )
            )
        for copy in group:
            copy.start()
        copies.append(group)
    first.wait()
    parts = jnp.concatenate(parts_of(r_ref[...], 3), axis=0)
    for piece in range(pieces):
        for copy in copies[piece]:
            copy.wait()
        at = rows_of(1 - ids_ref[0], piece, pieces, height)
        out_ref[piece] = raw_terms(parts, m_ref, g_ref, at) / replicas
    for group in copies[pieces:]:
        for copy in group:
            copy.wait()


def load(ids, momentum, grads, right_factor, pieces, replicas):
    rank, cols = right_factor.shape
    loops, rows = grads.shape[1:3]
    return pl.pallas_call(
        functools.partial(load_kernel, replicas),
        out_shape=[
            pltpu.VMEM(momentum.shape, momentum.dtype),
            pltpu.VMEM(grads.shape, grads.dtype),
            pltpu.VMEM((rank, cols), F32),
            jax.ShapeDtypeStruct((pieces, rank, rows // (2 * pieces)), F32),
        ],
        in_specs=[SMEM_SPEC] + [HBM_SPEC] * 3,
        out_specs=[VMEM_SPEC] * 4,
        scratch_shapes=[
            pltpu.SemaphoreType.DMA((2 * pieces, loops + 1)),
            pltpu.SemaphoreType.DMA,
        ],
        compiler_params=GRANT,
        name="load",
    )(ids, left_out(momentum), left_out(grads), left_out(right_factor))


def basis_kernel(r_ref, out_ref):
    out_ref[...] = inverse_lower(exact_dot(r_ref[...], r_ref[...], NT), 1e-5)


def basis(right_factor):
    rank = right_factor.shape[0]
    return pl.pallas_call(
        basis_kernel,
        out_shape=jax.ShapeDtypeStruct((rank, rank), F32),
        in_specs=[VMEM_SPEC],
        out_specs=VMEM_SPEC,
        compiler_params=GRANT,
        name="basis",
    )(held(right_factor))


def raw_kernel(replicas, ids_ref, m_ref, g_ref, r_ref, out_ref):
    pieces, _, height = out_ref.shape
    parts = jnp.concatenate(parts_of(r_ref[...], 3), axis=0)
    for piece in range(pieces):
        at = rows_of(ids_ref[0], piece, pieces, height)
        out_ref[piece] = raw_terms(parts, m_ref, g_ref, at) / replicas


def raw_half(ids, momentum, grads, right_factor, pieces, replicas):
    rank = right_factor.shape[0]
    height = grads.shape[2] // (2 * pieces)
    return pl.pallas_call(
        functools.partial(raw_kernel, replicas),
        out_shape=jax.ShapeDtypeStruct((pieces, rank, height), F32),
        in_specs=[SMEM_SPEC] + [VMEM_SPEC] * 3,
        out_specs=VMEM_SPEC,
        compiler_params=GRANT,
        name="raw_half",
    )(ids, held(momentum), held(grads), held(right_factor))


def products_kernel(
    size, ids_ref, basis_ref, own_ref, other_ref, m_ref, g_ref, left_ref, *rest
):
    sends, (pieces_ref,) = rest[:size], rest[size:]
    half, rank, height = own_ref.shape
    cols = m_ref.shape[2]
    total = gram = None
    for q in range(2 * half):
        piece = jnp.where(ids_ref[0] == q // half, own_ref[q % half], other_ref[q % half])
        piece = exact_dot(basis_ref[...], piece)
        left_ref[q] = piece
        parts = jnp.concatenate(parts_of(piece, 3), axis=0)
        at = slice(q * height, (q + 1) * height)
        more = dot(parts, m_ref[0, at, :])
        for i in range(g_ref.shape[1]):
            more += dot(parts, g_ref[0, i, at, :])
        total = more if total is None else total + more
        more = exact_dot(piece, piece, NT)
        gram = more if gram is None else gram + more
    total = total[:rank] + total[rank : 2 * rank] + total[2 * rank :]
    width = cols // size
    for j in range(size):
        pieces_ref[j] = total[:, j * width : (j + 1) * width]
    for s, send in enumerate(sends):
        send[:rank, :] = pieces_ref[jnp.bitwise_xor(ids_ref[1], s)]
        pack(send, gram)


def pack(ref, gram):
    rank = gram.shape[0]
    side = ref.shape[1] // rank
    height = rank // side
    for j in range(side):
        ref[rank:, j * rank : (j + 1) * rank] = gram[j * height : (j + 1) * height]


def packed_rows(rank, width):
    side = width // rank
    assert side * rank == width and rank % side == 0
    return rank + rank // side


def products(ids, base, own, other, momentum, grads, size):
    half, rank, height = own.shape
    width = grads.shape[3] // size
    return pl.pallas_call(
        functools.partial(products_kernel, size),
        out_shape=[jax.ShapeDtypeStruct((2 * half, rank, height), F32)]
        + [jax.ShapeDtypeStruct((packed_rows(rank, width), width), F32)] * size,
        in_specs=[SMEM_SPEC] + [VMEM_SPEC] * 5,
        out_specs=[VMEM_SPEC] * (1 + size),
        scratch_shapes=[pltpu.VMEM((size, rank, width), F32)],
        compiler_params=GRANT,
        name="products",
    )(ids, base, own, other, held(momentum), held(grads))


def gram_of(refs, rank):
    gram = refs[0][rank:, :]
    for ref in refs[1:]:
        gram = gram + ref[rank:, :]
    side = gram.shape[1] // rank
    return jnp.concatenate([gram[:, j * rank : (j + 1) * rank] for j in range(side)], axis=0)


def first_kernel(size, *refs):
    got, left_ref, step_ref, first_ref, send_ref = refs[:size], *refs[size:]
    rank = left_ref.shape[1]
    mine = got[0][:rank, :]
    for ref in got[1:]:
        mine = mine + ref[:rank, :]
    send_ref[:rank, :] = mine
    step = inverse_lower(gram_of(got, rank))
    step_ref[...] = step
    total = None
    for q in range(left_ref.shape[0]):
        first = exact_dot(step, left_ref[q])
        first_ref[q] = first
        more = exact_dot(first, first, NT)
        total = more if total is None else total + more
    pack(send_ref, total)


def first_sweep(got, left):
    rank = left.shape[1]
    return pl.pallas_call(
        functools.partial(first_kernel, len(got)),
        out_shape=[
            jax.ShapeDtypeStruct((rank, rank), F32),
            jax.ShapeDtypeStruct(left.shape, F32),
            jax.ShapeDtypeStruct(got[0].shape, F32),
        ],
        compiler_params=GRANT,
        name="first_sweep",
    )(*got, left)


def second_kernel(size, *refs):
    got, (step_ref, first_ref, left_ref, both_ref) = refs[:size], refs[size:]
    step = inverse_lower(gram_of(got, step_ref.shape[0]))
    for q in range(first_ref.shape[0]):
        left_ref[q] = exact_dot(step, first_ref[q])
    both_ref[...] = exact_dot(step, step_ref[...])


def second_sweep(got, step, first):
    return pl.pallas_call(
        functools.partial(second_kernel, len(got)),
        out_shape=[
            jax.ShapeDtypeStruct(first.shape, F32),
            jax.ShapeDtypeStruct(step.shape, F32),
        ],
        compiler_params=GRANT,
        name="second_sweep",
    )(*got, step, first)


def shared_kernel(size, replicas, ids_ref, both_ref, *refs):
    own, other, (shared_ref, sums_ref) = refs[:size], refs[size : 2 * size], refs[2 * size :]
    both = both_ref[...]
    sums = None
    for s in range(size):
        rank = both.shape[0]
        total = own[s][:rank, :] + other[s][:rank, :]
        shared = exact_dot(both, total) / replicas
        shared_ref[jnp.bitwise_xor(ids_ref[1], s)] = shared
        squares = shared * shared
        lanes = min(128, squares.shape[1])
        for at in range(0, squares.shape[1], lanes):
            more = squares[:, at : at + lanes]
            sums = more if sums is None else sums + more
    sums_ref[...] = sums


def shared_step(ids, both, own, other, replicas):
    size = len(own)
    rank, width = both.shape[0], own[0].shape[1]
    return pl.pallas_call(
        functools.partial(shared_kernel, size, replicas),
        out_shape=[
            jax.ShapeDtypeStruct((size, rank, width), F32),
            jax.ShapeDtypeStruct((rank, min(128, width)), F32),
        ],
        in_specs=[SMEM_SPEC] + [VMEM_SPEC] * (1 + 2 * size),
        out_specs=[VMEM_SPEC] * 2,
        compiler_params=GRANT,
        name="shared_step",
    )(ids, both, *own, *other)


def tall(x):
    hi, lo = parts_of(x, 2)
    return jnp.concatenate([hi, lo, hi, lo], axis=0)


def wide(x):
    hi, lo = parts_of(x, 2)
    return jnp.concatenate([hi, hi, lo, lo], axis=0)


def blend_kernel(m_ref, g_ref, out_ref):
    blended = g_ref[0, 0].astype(F32)
    for i in range(1, g_ref.shape[1]):
        blended = blended + g_ref[0, i].astype(F32)
    out_ref[...] = m_ref[0].astype(F32) + blended


def blend(momentum, grads):
    return pl.pallas_call(
        blend_kernel,
        out_shape=pltpu.VMEM(momentum.shape[1:], F32),
        in_specs=[VMEM_SPEC] * 2,
        out_specs=VMEM_SPEC,
        compiler_params=GRANT,
        name="blend",
    )(held(momentum), held(grads))


def momentum_kernel(size, ids_ref, left_ref, both_ref, *refs):
    own, refs = refs[:size], refs[size:]
    blended_ref, out_ref, right_ref, slots_ref, sems = refs
    both = decay_part * both_ref[...]
    for s in range(size):
        right_ref[jnp.bitwise_xor(ids_ref[1], s)] = wide(
            exact_dot(both, own[s][: both.shape[0], :])
        )
    width = right_ref.shape[2]
    pieces, _, height = left_ref.shape
    copies = []
    for q in range(pieces):
        left = tall(left_ref[q])
        down = slice(q * height, (q + 1) * height)
        for j in range(size):
            at = slice(j * width, (j + 1) * width)
            projected = dot(left, right_ref[j], TN)
            slots_ref[q, :, at] = (blended_ref[down, at] - projected).astype(BF16)
        copies.append(
            pltpu.make_async_copy(slots_ref.at[q], out_ref.at[0, down, :], sems.at[q])
        )
        copies[-1].start()
    for copy in copies:
        copy.wait()


def momentum_step(ids, left, both, own, blended):
    size = len(own)
    pieces, rank, height = left.shape
    width = own[0].shape[1]
    rows, cols = blended.shape
    return pl.pallas_call(
        functools.partial(momentum_kernel, size),
        out_shape=jax.ShapeDtypeStruct((1, rows, cols), BF16),
        in_specs=[SMEM_SPEC] + [VMEM_SPEC] * (3 + size),
        out_specs=HBM_SPEC,
        scratch_shapes=[
            pltpu.VMEM((size, 4 * rank, width), BF16),
            pltpu.VMEM((pieces, height, cols), BF16),
            pltpu.SemaphoreType.DMA((pieces,)),
        ],
        compiler_params=GRANT,
        name="momentum_step",
    )(ids, left, both, *own, held(blended))


def weight_kernel(count, scale, left_ref, shared_ref, *refs):
    sums, refs = refs[:count], refs[count:]
    w_ref, out_ref, new_right_out, new_right_ref, right_ref, slots_ref, sems = refs
    size, _, width = right_ref.shape
    total = sums[0][...]
    for ref in sums[1:]:
        total = total + ref[...]
    norm = jnp.sqrt(jnp.sum(total, axis=1, keepdims=True) + epsilon)
    for j in range(size):
        new_right = shared_ref[j] / norm
        new_right_ref[:, j * width : (j + 1) * width] = new_right
        right_ref[j] = wide(scale * new_right)
    pieces, _, height = left_ref.shape
    copies = [pltpu.make_async_copy(new_right_ref, new_right_out, sems.at[pieces])]
    copies[-1].start()
    for q in range(pieces):
        left = tall(left_ref[q])
        down = slice(q * height, (q + 1) * height)
        for j in range(size):
            at = slice(j * width, (j + 1) * width)
            slots_ref[q, :, at] = w_ref[down, at] - dot(left, right_ref[j], TN)
        copies.append(pltpu.make_async_copy(slots_ref.at[q], out_ref.at[down, :], sems.at[q]))
        copies[-1].start()
    for copy in copies:
        copy.wait()


def weight_step(left, shared, sums, weight, scale):
    pieces, rank, height = left.shape
    size, _, width = shared.shape
    _, cols = weight.shape
    return pl.pallas_call(
        functools.partial(weight_kernel, len(sums), scale),
        out_shape=[
            jax.ShapeDtypeStruct(weight.shape, F32),
            jax.ShapeDtypeStruct((rank, cols), F32),
        ],
        in_specs=[VMEM_SPEC] * (3 + len(sums)),
        out_specs=[HBM_SPEC, HBM_SPEC],
        scratch_shapes=[
            pltpu.VMEM((rank, cols), F32),
            pltpu.VMEM((size, 4 * rank, width), BF16),
            pltpu.VMEM((pieces, height, cols), F32),
            pltpu.SemaphoreType.DMA((pieces + 1,)),
        ],
        compiler_params=GRANT,
        name="weight_step",
    )(left, shared, *sums, held(weight))


def swap(x, axis, bit):
    size = lax.axis_size(axis)
    return lax.ppermute(x, axis, [(i, i ^ bit) for i in range(size)])


def bits_of(axis):
    size = lax.axis_size(axis)
    assert size & (size - 1) == 0
    return [(axis, 1 << i) for i in range(size.bit_length() - 1)]


def half_pairs():
    count = lax.axis_size("tensor")
    bits = [bit for _, bit in bits_of("tensor")[1:]] + [bit * count for _, bit in bits_of("dp")]
    every = range(count * lax.axis_size("dp"))
    return [
        [(i, i ^ (bits[-1 - stage] if i % 2 else bits[stage])) for i in every]
        for stage in range(len(bits))
    ]


def step(weight, momentum, grads, right_factor):
    replicas = lax.axis_size("dp")
    size = lax.axis_size("fsdp")
    others = range(1, size)
    rank = right_factor.shape[0]
    near = lax.axis_index("tensor") % 2
    ids = jnp.stack([near, lax.axis_index("fsdp")]).astype(jnp.int32)

    momentum, grads, right_factor, sent = load(
        ids, momentum, grads, right_factor, 2, replicas
    )
    sent = swap(sent, "tensor", 1)
    kept = raw_half(ids, momentum, grads, right_factor, 2, replicas)
    own = kept + sent
    right_factor, own = lax.optimization_barrier((right_factor, own))
    base = basis(right_factor)
    for pairs in half_pairs():
        own_in = lax.ppermute(own, ("dp", "tensor"), pairs)
        own = own + own_in
    other = swap(own, "tensor", 1)

    left_raw, *sends = products(ids, base, own, other, momentum, grads, size)
    blended = blend(momentum, grads)
    got = [sends[0]] + [swap(sends[s], "fsdp", s) for s in others]
    weight, left_raw = lax.optimization_barrier((weight, left_raw))
    factor, first, send = first_sweep(got, left_raw)
    pieces = [send] + [swap(send, "fsdp", s) for s in others]

    ours, theirs = [], []
    for piece in pieces:
        piece = piece[:rank]
        for axis, bit in bits_of("dp")[:-1]:
            piece = piece + swap(piece, axis, bit)
        ours.append(piece)
        theirs.append(swap(piece, *bits_of("dp")[-1]))

    left, both = second_sweep(pieces, factor, first)
    shared, sums = shared_step(ids, both, ours, theirs, replicas)
    sums_all = [sums] + [swap(sums, "tensor", s) for s in range(1, lax.axis_size("tensor"))]
    new_momentum = momentum_step(ids, left, both, pieces, blended)
    scale = learn_rate * math.sqrt(ROWS / COLS)
    new_weight, new_right = weight_step(left, shared, sums_all, weight, scale)
    return (new_weight, new_momentum, new_right)


def solution(mesh):
    placed = (
        P("fsdp", "tensor"),
        P("dp", "fsdp", "tensor"),
        P("dp", None, "fsdp", "tensor"),
        P(None, "tensor"),
    )
    return jax.shard_map(
        step,
        mesh=mesh,
        in_specs=placed,
        out_specs=(P("fsdp", "tensor"), P("dp", "fsdp", "tensor"), P(None, "tensor")),
        check_vma=False,
    )
```

```python
import functools
import math

import jax
import jax.numpy as jnp
from jax import lax
from jax.experimental import pallas as pl
from jax.experimental.pallas import tpu as pltpu
from jax.sharding import PartitionSpec as P


ROWS = 4096
COLS = 4096

decay_part = 0.05
learn_rate = 0.02
epsilon = 1e-06

F32 = jnp.float32
BF16 = jnp.bfloat16
NT = (((1,), (1,)), ((), ()))
NN = (((1,), (0,)), ((), ()))
TN = (((0,), (0,)), ((), ()))


def dot(a, b, dims=NN):
    return lax.dot_general(a, b, dims, preferred_element_type=F32)


def exact_dot(a, b, dims=NN):
    return lax.dot_general(
        a, b, dims, precision=lax.Precision.HIGHEST, preferred_element_type=F32
    )


def parts_of(x, count):
    parts = []
    for _ in range(count):
        part = x.astype(BF16)
        parts.append(part)
        x = x - part.astype(F32)
    return parts


def inverse_lower(gram, floor=None):
    rank = gram.shape[0]
    rows = lax.broadcasted_iota(jnp.int32, (rank, rank), 0)
    cols = lax.broadcasted_iota(jnp.int32, (rank, rank), 1)
    unit = jnp.where(rows == cols, 1.0, 0.0).astype(F32)
    both = jnp.concatenate([unit, gram], axis=1)
    height = 8
    full = (height, 2 * rank)
    blocks = [both[i : i + height] for i in range(0, rank, height)]
    sub = lax.broadcasted_iota(jnp.int32, full, 0)

    def spread(x, s):
        return jnp.broadcast_to(x[s : s + 1, :], full)

    if floor is not None:
        least = floor * jnp.sum(jnp.where(rows == cols, gram, 0.0), axis=1, keepdims=True)
        least = jnp.broadcast_to(least, (rank, 2 * rank))

    pivots = []
    for at in range(rank // height):
        live = blocks[at:]
        columns = []
        for j in range(height):
            k = rank + at * height + j
            columns.append(
                [jnp.where(sub >= 0, jnp.broadcast_to(x[:, k : k + 1], full), 0.0) for x in live]
            )
        found = jnp.ones(full, F32)
        for k in range(height):
            pivot = spread(columns[k][0], k)
            if floor is not None:
                pivot = jnp.maximum(pivot, spread(least[at * height : (at + 1) * height], k))
            found = jnp.where(sub == k, pivot, found)
            over = 1.0 / pivot
            line = spread(live[0], k) * over
            for j in range(k + 1, height):
                more = spread(columns[j][0], k) * over
                for i in range(len(live)):
                    columns[j][i] = columns[j][i] - columns[k][i] * more
            for i in range(len(live)):
                column = columns[k][i]
                if i == 0:
                    if k == height - 1:
                        continue
                    column = jnp.where(sub > k, column, 0.0)
                live[i] = live[i] - column * line
        blocks[at:] = live
        pivots.append(found)
    both = jnp.concatenate(blocks, axis=0)
    return both[:, :rank] / jnp.sqrt(jnp.concatenate(pivots, axis=0)[:, :rank])


VMEM_SPEC = pl.BlockSpec(memory_space=pltpu.VMEM)
SMEM_SPEC = pl.BlockSpec(memory_space=pltpu.SMEM)
HBM_SPEC = pl.BlockSpec(memory_space=pltpu.HBM)


GRANT = pltpu.CompilerParams(vmem_limit_bytes=20 * 1024 * 1024)


def left_out(x):
    return pltpu.with_memory_space_constraint(x, pltpu.HBM)


def held(x):
    return pltpu.with_memory_space_constraint(x, pltpu.VMEM)


def raw_terms(parts, m_ref, g_ref, at):
    rank = parts.shape[0] // 3
    total = dot(parts, m_ref[0, at, :], NT)
    for i in range(g_ref.shape[1]):
        total += dot(parts, g_ref[0, i, at, :], NT)
    return total[:rank] + total[rank : 2 * rank] + total[2 * rank :]


def rows_of(half, piece, pieces, height):
    return pl.ds(pl.multiple_of((half * pieces + piece) * height, height), height)


def load_kernel(
    replicas, ids_ref, m_hbm, g_hbm, r_hbm, m_ref, g_ref, r_ref, out_ref, sems, r_sem
):
    pieces, _, height = out_ref.shape
    loops = g_hbm.shape[1]
    first = pltpu.make_async_copy(r_hbm, r_ref, r_sem)
    first.start()
    copies = []
    for piece in range(2 * pieces):
        half = ids_ref[0] if piece >= pieces else 1 - ids_ref[0]
        at = rows_of(half, piece % pieces, pieces, height)
        group = [
            pltpu.make_async_copy(m_hbm.at[0, at, :], m_ref.at[0, at, :], sems.at[piece, loops])
        ]
        for i in range(loops):
            group.append(
                pltpu.make_async_copy(
                    g_hbm.at[0, i, at, :], g_ref.at[0, i, at, :], sems.at[piece, i]
                )
            )
        for copy in group:
            copy.start()
        copies.append(group)
    first.wait()
    parts = jnp.concatenate(parts_of(r_ref[...], 3), axis=0)
    for piece in range(pieces):
        for copy in copies[piece]:
            copy.wait()
        at = rows_of(1 - ids_ref[0], piece, pieces, height)
        out_ref[piece] = raw_terms(parts, m_ref, g_ref, at) / replicas
    for group in copies[pieces:]:
        for copy in group:
            copy.wait()


def load(ids, momentum, grads, right_factor, pieces, replicas):
    rank, cols = right_factor.shape
    loops, rows = grads.shape[1:3]
    return pl.pallas_call(
        functools.partial(load_kernel, replicas),
        out_shape=[
            pltpu.VMEM(momentum.shape, momentum.dtype),
            pltpu.VMEM(grads.shape, grads.dtype),
            pltpu.VMEM((rank, cols), F32),
            jax.ShapeDtypeStruct((pieces, rank, rows // (2 * pieces)), F32),
        ],
        in_specs=[SMEM_SPEC] + [HBM_SPEC] * 3,
        out_specs=[VMEM_SPEC] * 4,
        scratch_shapes=[
            pltpu.SemaphoreType.DMA((2 * pieces, loops + 1)),
            pltpu.SemaphoreType.DMA,
        ],
        compiler_params=GRANT,
        name="load",
    )(ids, left_out(momentum), left_out(grads), left_out(right_factor))


def basis_kernel(r_ref, out_ref):
    out_ref[...] = inverse_lower(exact_dot(r_ref[...], r_ref[...], NT), 1e-5)


def basis(right_factor):
    rank = right_factor.shape[0]
    return pl.pallas_call(
        basis_kernel,
        out_shape=jax.ShapeDtypeStruct((rank, rank), F32),
        in_specs=[VMEM_SPEC],
        out_specs=VMEM_SPEC,
        compiler_params=GRANT,
        name="basis",
    )(held(right_factor))


def raw_kernel(replicas, ids_ref, m_ref, g_ref, r_ref, out_ref):
    pieces, _, height = out_ref.shape
    parts = jnp.concatenate(parts_of(r_ref[...], 3), axis=0)
    for piece in range(pieces):
        at = rows_of(ids_ref[0], piece, pieces, height)
        out_ref[piece] = raw_terms(parts, m_ref, g_ref, at) / replicas


def raw_half(ids, momentum, grads, right_factor, pieces, replicas):
    rank = right_factor.shape[0]
    height = grads.shape[2] // (2 * pieces)
    return pl.pallas_call(
        functools.partial(raw_kernel, replicas),
        out_shape=jax.ShapeDtypeStruct((pieces, rank, height), F32),
        in_specs=[SMEM_SPEC] + [VMEM_SPEC] * 3,
        out_specs=VMEM_SPEC,
        compiler_params=GRANT,
        name="raw_half",
    )(ids, held(momentum), held(grads), held(right_factor))


def products_kernel(
    size, ids_ref, basis_ref, own_ref, other_ref, m_ref, g_ref, left_ref, *rest
):
    sends, (pieces_ref,) = rest[:size], rest[size:]
    half, rank, height = own_ref.shape
    cols = m_ref.shape[2]
    total = gram = None
    for q in range(2 * half):
        piece = jnp.where(ids_ref[0] == q // half, own_ref[q % half], other_ref[q % half])
        piece = exact_dot(basis_ref[...], piece)
        left_ref[q] = piece
        parts = jnp.concatenate(parts_of(piece, 3), axis=0)
        at = slice(q * height, (q + 1) * height)
        more = dot(parts, m_ref[0, at, :])
        for i in range(g_ref.shape[1]):
            more += dot(parts, g_ref[0, i, at, :])
        total = more if total is None else total + more
        more = exact_dot(piece, piece, NT)
        gram = more if gram is None else gram + more
    total = total[:rank] + total[rank : 2 * rank] + total[2 * rank :]
    width = cols // size
    for j in range(size):
        pieces_ref[j] = total[:, j * width : (j + 1) * width]
    for s, send in enumerate(sends):
        send[:rank, :] = pieces_ref[jnp.bitwise_xor(ids_ref[1], s)]
        pack(send, gram)


def pack(ref, gram):
    rank = gram.shape[0]
    side = ref.shape[1] // rank
    height = rank // side
    for j in range(side):
        ref[rank:, j * rank : (j + 1) * rank] = gram[j * height : (j + 1) * height]


def packed_rows(rank, width):
    side = width // rank
    assert side * rank == width and rank % side == 0
    return rank + rank // side


def products(ids, base, own, other, momentum, grads, size):
    half, rank, height = own.shape
    width = grads.shape[3] // size
    return pl.pallas_call(
        functools.partial(products_kernel, size),
        out_shape=[jax.ShapeDtypeStruct((2 * half, rank, height), F32)]
        + [jax.ShapeDtypeStruct((packed_rows(rank, width), width), F32)] * size,
        in_specs=[SMEM_SPEC] + [VMEM_SPEC] * 5,
        out_specs=[VMEM_SPEC] * (1 + size),
        scratch_shapes=[pltpu.VMEM((size, rank, width), F32)],
        compiler_params=GRANT,
        name="products",
    )(ids, base, own, other, held(momentum), held(grads))


def gram_of(refs, rank):
    gram = refs[0][rank:, :]
    for ref in refs[1:]:
        gram = gram + ref[rank:, :]
    side = gram.shape[1] // rank
    return jnp.concatenate([gram[:, j * rank : (j + 1) * rank] for j in range(side)], axis=0)


def first_kernel(size, *refs):
    got, left_ref, step_ref, first_ref, send_ref = refs[:size], *refs[size:]
    rank = left_ref.shape[1]
    mine = got[0][:rank, :]
    for ref in got[1:]:
        mine = mine + ref[:rank, :]
    send_ref[:rank, :] = mine
    step = inverse_lower(gram_of(got, rank))
    step_ref[...] = step
    total = None
    for q in range(left_ref.shape[0]):
        first = exact_dot(step, left_ref[q])
        first_ref[q] = first
        more = exact_dot(first, first, NT)
        total = more if total is None else total + more
    pack(send_ref, total)


def first_sweep(got, left):
    rank = left.shape[1]
    return pl.pallas_call(
        functools.partial(first_kernel, len(got)),
        out_shape=[
            jax.ShapeDtypeStruct((rank, rank), F32),
            jax.ShapeDtypeStruct(left.shape, F32),
            jax.ShapeDtypeStruct(got[0].shape, F32),
        ],
        compiler_params=GRANT,
        name="first_sweep",
    )(*got, left)


def second_kernel(size, *refs):
    got, (step_ref, first_ref, left_ref, both_ref) = refs[:size], refs[size:]
    step = inverse_lower(gram_of(got, step_ref.shape[0]))
    for q in range(first_ref.shape[0]):
        left_ref[q] = exact_dot(step, first_ref[q])
    both_ref[...] = exact_dot(step, step_ref[...])


def second_sweep(got, step, first):
    return pl.pallas_call(
        functools.partial(second_kernel, len(got)),
        out_shape=[
            jax.ShapeDtypeStruct(first.shape, F32),
            jax.ShapeDtypeStruct(step.shape, F32),
        ],
        compiler_params=GRANT,
        name="second_sweep",
    )(*got, step, first)


def shared_kernel(size, replicas, ids_ref, both_ref, *refs):
    own, other, (shared_ref, sums_ref) = refs[:size], refs[size : 2 * size], refs[2 * size :]
    both = both_ref[...]
    sums = None
    for s in range(size):
        rank = both.shape[0]
        total = own[s][:rank, :] + other[s][:rank, :]
        shared = exact_dot(both, total) / replicas
        shared_ref[jnp.bitwise_xor(ids_ref[1], s)] = shared
        squares = shared * shared
        lanes = min(128, squares.shape[1])
        for at in range(0, squares.shape[1], lanes):
            more = squares[:, at : at + lanes]
            sums = more if sums is None else sums + more
    sums_ref[...] = sums


def shared_step(ids, both, own, other, replicas):
    size = len(own)
    rank, width = both.shape[0], own[0].shape[1]
    return pl.pallas_call(
        functools.partial(shared_kernel, size, replicas),
        out_shape=[
            jax.ShapeDtypeStruct((size, rank, width), F32),
            jax.ShapeDtypeStruct((rank, min(128, width)), F32),
        ],
        in_specs=[SMEM_SPEC] + [VMEM_SPEC] * (1 + 2 * size),
        out_specs=[VMEM_SPEC] * 2,
        compiler_params=GRANT,
        name="shared_step",
    )(ids, both, *own, *other)


def tall(x):
    hi, lo = parts_of(x, 2)
    return jnp.concatenate([hi, lo, hi, lo], axis=0)


def wide(x):
    hi, lo = parts_of(x, 2)
    return jnp.concatenate([hi, hi, lo, lo], axis=0)


def blend_kernel(m_ref, g_ref, out_ref):
    blended = g_ref[0, 0].astype(F32)
    for i in range(1, g_ref.shape[1]):
        blended = blended + g_ref[0, i].astype(F32)
    out_ref[...] = m_ref[0].astype(F32) + blended


def blend(momentum, grads):
    return pl.pallas_call(
        blend_kernel,
        out_shape=pltpu.VMEM(momentum.shape[1:], F32),
        in_specs=[VMEM_SPEC] * 2,
        out_specs=VMEM_SPEC,
        compiler_params=GRANT,
        name="blend",
    )(held(momentum), held(grads))


def factors_kernel(size, ids_ref, left_ref, both_ref, *refs):
    own, (tall_ref, right_ref) = refs[:size], refs[size:]
    both = decay_part * both_ref[...]
    for s in range(size):
        right_ref[jnp.bitwise_xor(ids_ref[1], s)] = wide(
            exact_dot(both, own[s][: both.shape[0], :])
        )
    for q in range(left_ref.shape[0]):
        tall_ref[q] = tall(left_ref[q])


def factors(ids, left, both, own):
    size = len(own)
    pieces, rank, height = left.shape
    return pl.pallas_call(
        functools.partial(factors_kernel, size),
        out_shape=[
            jax.ShapeDtypeStruct((pieces, 4 * rank, height), BF16),
            jax.ShapeDtypeStruct((size, 4 * rank, own[0].shape[1]), BF16),
        ],
        in_specs=[SMEM_SPEC] + [VMEM_SPEC] * (2 + size),
        out_specs=[VMEM_SPEC] * 2,
        compiler_params=GRANT,
        name="factors",
    )(ids, left, both, *own)


def momentum_kernel(left_ref, right_ref, blended_ref, out_ref, slots_ref, sems):
    size, _, width = right_ref.shape
    pieces, _, height = left_ref.shape
    copies = []
    for q in range(pieces):
        left = left_ref[q]
        down = slice(q * height, (q + 1) * height)
        for j in range(size):
            at = slice(j * width, (j + 1) * width)
            projected = dot(left, right_ref[j], TN)
            slots_ref[q, :, at] = (blended_ref[down, at] - projected).astype(BF16)
            send_out(copies, slots_ref, out_ref.at[0], sems, q, j, size)
    for copy in copies:
        copy.wait()


def send_out(copies, slots_ref, out_ref, sems, q, j, size):
    height, cols = slots_ref.shape[1:]
    half = size // 2
    if (j + 1) % half:
        return
    side = j // half
    at = pl.ds(side * (cols // 2), cols // 2)
    copies.append(
        pltpu.make_async_copy(
            slots_ref.at[q, :, at],
            out_ref.at[pl.ds(q * height, height), at],
            sems.at[2 * q + side],
        )
    )
    copies[-1].start()


def momentum_step(left, right, blended):
    pieces, _, height = left.shape
    rows, cols = blended.shape
    return pl.pallas_call(
        momentum_kernel,
        out_shape=jax.ShapeDtypeStruct((1, rows, cols), BF16),
        in_specs=[VMEM_SPEC] * 3,
        out_specs=HBM_SPEC,
        scratch_shapes=[
            pltpu.VMEM((pieces, height, cols), BF16),
            pltpu.SemaphoreType.DMA((2 * pieces,)),
        ],
        compiler_params=GRANT,
        name="momentum_step",
    )(left, right, held(blended))


def weight_kernel(count, scale, left_ref, shared_ref, *refs):
    sums, refs = refs[:count], refs[count:]
    w_ref, out_ref, new_right_out, new_right_ref, right_ref, slots_ref, sems = refs
    size, _, width = right_ref.shape
    total = sums[0][...]
    for ref in sums[1:]:
        total = total + ref[...]
    norm = jnp.sqrt(jnp.sum(total, axis=1, keepdims=True) + epsilon)
    for j in range(size):
        new_right = shared_ref[j] / norm
        new_right_ref[:, j * width : (j + 1) * width] = new_right
        right_ref[j] = wide(scale * new_right)
    pieces, _, height = left_ref.shape
    copies = [pltpu.make_async_copy(new_right_ref, new_right_out, sems.at[2 * pieces])]
    copies[-1].start()
    for q in range(pieces):
        left = left_ref[q]
        down = slice(q * height, (q + 1) * height)
        for j in range(size):
            at = slice(j * width, (j + 1) * width)
            slots_ref[q, :, at] = w_ref[down, at] - dot(left, right_ref[j], TN)
            send_out(copies, slots_ref, out_ref, sems, q, j, size)
    for copy in copies:
        copy.wait()


def weight_step(left, shared, sums, weight, scale):
    pieces, _, height = left.shape
    size, rank, width = shared.shape
    _, cols = weight.shape
    return pl.pallas_call(
        functools.partial(weight_kernel, len(sums), scale),
        out_shape=[
            jax.ShapeDtypeStruct(weight.shape, F32),
            jax.ShapeDtypeStruct((rank, cols), F32),
        ],
        in_specs=[VMEM_SPEC] * (3 + len(sums)),
        out_specs=[HBM_SPEC, HBM_SPEC],
        scratch_shapes=[
            pltpu.VMEM((rank, cols), F32),
            pltpu.VMEM((size, 4 * rank, width), BF16),
            pltpu.VMEM((pieces, height, cols), F32),
            pltpu.SemaphoreType.DMA((2 * pieces + 1,)),
        ],
        compiler_params=GRANT,
        name="weight_step",
    )(left, shared, *sums, held(weight))


def swap(x, axis, bit):
    size = lax.axis_size(axis)
    return lax.ppermute(x, axis, [(i, i ^ bit) for i in range(size)])


def bits_of(axis):
    size = lax.axis_size(axis)
    assert size & (size - 1) == 0
    return [(axis, 1 << i) for i in range(size.bit_length() - 1)]


def half_pairs():
    count = lax.axis_size("tensor")
    bits = [bit for _, bit in bits_of("tensor")[1:]] + [bit * count for _, bit in bits_of("dp")]
    every = range(count * lax.axis_size("dp"))
    return [
        [(i, i ^ (bits[-1 - stage] if i % 2 else bits[stage])) for i in every]
        for stage in range(len(bits))
    ]


def step(weight, momentum, grads, right_factor):
    replicas = lax.axis_size("dp")
    size = lax.axis_size("fsdp")
    others = range(1, size)
    rank = right_factor.shape[0]
    near = lax.axis_index("tensor") % 2
    ids = jnp.stack([near, lax.axis_index("fsdp")]).astype(jnp.int32)

    momentum, grads, right_factor, sent = load(
        ids, momentum, grads, right_factor, 2, replicas
    )
    sent = swap(sent, "tensor", 1)
    kept = raw_half(ids, momentum, grads, right_factor, 2, replicas)
    own = kept + sent
    right_factor, own = lax.optimization_barrier((right_factor, own))
    base = basis(right_factor)
    for pairs in half_pairs():
        own_in = lax.ppermute(own, ("dp", "tensor"), pairs)
        own = own + own_in
    other = swap(own, "tensor", 1)

    left_raw, *sends = products(ids, base, own, other, momentum, grads, size)
    blended = blend(momentum, grads)
    got = [sends[0]] + [swap(sends[s], "fsdp", s) for s in others]
    weight, left_raw = lax.optimization_barrier((weight, left_raw))
    factor, first, send = first_sweep(got, left_raw)
    pieces = [send] + [swap(send, "fsdp", s) for s in others]

    ours, theirs = [], []
    for piece in pieces:
        piece = piece[:rank]
        for axis, bit in bits_of("dp")[:-1]:
            piece = piece + swap(piece, axis, bit)
        ours.append(piece)
        theirs.append(swap(piece, *bits_of("dp")[-1]))

    left, both = second_sweep(pieces, factor, first)
    left_parts, right_parts = factors(ids, left, both, pieces)
    shared, sums = shared_step(ids, both, ours, theirs, replicas)
    sums_all = [sums] + [swap(sums, "tensor", s) for s in range(1, lax.axis_size("tensor"))]
    new_momentum = momentum_step(left_parts, right_parts, blended)
    scale = learn_rate * math.sqrt(ROWS / COLS)
    new_weight, new_right = weight_step(left_parts, shared, sums_all, weight, scale)
    return (new_weight, new_momentum, new_right)


def solution(mesh):
    placed = (
        P("fsdp", "tensor"),
        P("dp", "fsdp", "tensor"),
        P("dp", None, "fsdp", "tensor"),
        P(None, "tensor"),
    )
    return jax.shard_map(
        step,
        mesh=mesh,
        in_specs=placed,
        out_specs=(P("fsdp", "tensor"), P("dp", "fsdp", "tensor"), P(None, "tensor")),
        check_vma=False,
    )
```
